32 devices in a mesh: group: 2 (over y), tm: 4 (over x, core), space: 4 (over z).
Axes of the slice: x: 2, y: 2, z: 4, core: 2. Of those that a mesh axis runs over, the one named last changes fastest.
Arguments:
- start_latent: float32 [32, 32, 256], P('group', 'space'), parts along dimension 0, may hold values from -6 to 6
- time_embed: float32 [8, 128], P('tm'), may hold values from -6 to 6
- drift_x: float32 [8], P('tm'), may hold values from -0.06 to -0.01
- drift_eps: float32 [8], P('tm'), may hold values from 0.02 to 0.1
- w_in: float32 [3, 3, 128, 16], replicated, may hold values from -0.5 to 0.5
- b_in: float32 [128], replicated, may hold values from -3 to 3
- w_mid: float32 [3, 3, 128, 128], replicated, may hold values from -0.1875 to 0.1875
- b_mid: float32 [128], replicated, may hold values from -3 to 3
- w_out: float32 [3, 3, 16, 128], replicated, may hold values from -0.1875 to 0.1875
- b_out: float32 [16], replicated, may hold values from -3 to 3
Outputs:
- trajectory: float32 [8, 32, 32, 256], P('tm', 'group', 'space'), parts along dimension 1
The draws below stay inside these ranges and needn't reach their ends.
There are 2 independent parts, one for each index of `group`. The reference program is written for one: setup_inputs(seed, part) draws one part's arguments, and reference() takes and returns one part's arrays. A program takes and returns all parts, laid end to end along the dimension named above; an argument that names none is the same for every part. Nothing has to cross between parts.
All inputs are finite; a program needn't handle non-finite values.
Results may differ from the reference program's by a relative error of at most 0.0001.
Values sent between devices are 32-bit elements; how exact they have to be, the bound alone decides.
A program may use at most 64 MiB of HBM per device.

```python
import math
import jax
import jax.numpy as jnp
from jax import lax

C = 16
HID = 128
COLS = 256
ITERS = 2
STATES = 8
HEIGHT = 32


def block_levels(stream_key, shape, split, smallest, top_value):
    def one(dim, blocks):
        heights = jax.random.uniform(jax.random.fold_in(jax.random.fold_in(stream_key, 6), dim), (blocks,), jnp.float32, smallest / len(split), top_value / len(split))
        return jnp.repeat(jnp.exp(heights), shape[dim] // blocks).reshape((-1,) + (1,) * (len(shape) - dim - 1))

    level = one(*split[0])
    for cut in split[1:]:
        level = level * one(*cut)
    return level


def bell_draw(rng, shape, scale, limit, cuts=(), held_as=jnp.bfloat16):
    loudness = block_levels(rng, shape, cuts, -0.22, 0.18) if cuts else 1.0
    array = jax.random.normal(rng, shape, jnp.float32) * scale * loudness
    return jnp.minimum(jnp.maximum(array, -limit), limit).astype(held_as)


def setup_inputs(seed: int = 0, part: int = 0) -> dict:
    key_list = jax.random.split(jax.random.key(seed), 11)
    own_keys = jax.random.split(jax.random.fold_in(key_list[10], part), 11)
    return {
        "start_latent": bell_draw(own_keys[0], (C, HEIGHT, COLS), 1.0, 6.0, ((1, 4),), jnp.float32),
        "time_embed": bell_draw(key_list[1], (STATES, HID), 1.0, 6.0, ((0, 4),), jnp.float32),
        "drift_x": jnp.clip(-0.06 + 0.04999999888241291 * jax.random.uniform(key_list[2], (STATES,), jnp.float32) ** block_levels(key_list[2], (STATES,), ((0, 4),), -0.2, 0.2), -0.06, -0.01),
        "drift_eps": jnp.clip(jnp.exp(math.log(0.1) - 1.609438 * jax.random.uniform(key_list[3], (STATES,), jnp.float32) ** block_levels(key_list[3], (STATES,), ((0, 4),), -0.2, 0.2)), 0.02, 0.1),
        "w_in": bell_draw(key_list[4], (3, 3, HID, C), (9 * C) ** -0.5, 0.5, (), jnp.float32),
        "b_in": bell_draw(key_list[5], (HID,), 0.5, 3.0, (), jnp.float32),
        "w_mid": bell_draw(key_list[6], (3, 3, HID, HID), (9 * HID) ** -0.5, 0.1875, (), jnp.float32),
        "b_mid": bell_draw(key_list[7], (HID,), 0.5, 3.0, (), jnp.float32),
        "w_out": bell_draw(key_list[8], (3, 3, C, HID), (9 * HID) ** -0.5, 0.1875, (), jnp.float32),
        "b_out": bell_draw(key_list[9], (C,), 0.5, 3.0, (), jnp.float32),
    }


def convolve(field, weight):
    kernel = jnp.transpose(weight, (2, 3, 0, 1))
    result = lax.conv_general_dilated(field[None], kernel, (1, 1), ((1, 1), (1, 1)), dimension_numbers=("NCHW", "OIHW", "NCHW"), precision=lax.Precision.HIGHEST)
    return result[0]


def reference(start_latent, time_embed, drift_x, drift_eps, w_in, b_in, w_mid, b_mid, w_out, b_out):
    def denoise_state(operands):
        field, embedding = operands
        first_hidden = jax.nn.silu(convolve(field, w_in) + (b_in + embedding)[:, None, None])
        second_hidden = jax.nn.silu(convolve(first_hidden, w_mid) + b_mid[:, None, None])
        return convolve(second_hidden, w_out) + b_out[:, None, None]

    trajectory = jnp.broadcast_to(start_latent[None], (STATES,) + start_latent.shape)
    for iteration in range(ITERS):
        inputs = jnp.concatenate([start_latent[None], trajectory[:-1]], 0)
        noise_pred = lax.map(denoise_state, (inputs, time_embed))
        drift = drift_x[:, None, None, None] * inputs + drift_eps[:, None, None, None] * noise_pred
        trajectory = start_latent[None] + jnp.cumsum(drift, 0)
    return trajectory
```

```python
import functools
import jax
import jax.numpy as jnp
from jax import lax
from jax.experimental import pallas as pl
from jax.experimental.pallas import tpu as pltpu
from jax.sharding import PartitionSpec as P

ITERS = 2
HALO = 3
BF = jnp.bfloat16
F32 = jnp.float32


def split(v):
    hi = v.astype(BF)
    lo = (v - hi.astype(F32)).astype(BF)
    return hi, lo


def shifted(v):
    cols = v.shape[1]
    lane = lax.broadcasted_iota(jnp.int32, v.shape, 1)
    left = jnp.where(lane == 0, 0.0, pltpu.roll(v, 1, 1))
    right = jnp.where(lane == cols - 1, 0.0, pltpu.roll(v, cols - 1, 1))
    return left, v, right


def dot(a, b):
    return jnp.dot(a, b, preferred_element_type=F32)


def silu(u):
    half = 0.5 * u
    return half + half * jnp.tanh(half)


def column(row, n):
    return jnp.transpose(jnp.broadcast_to(row, (n, row.shape[1])))


def wide(m, cols):
    return jnp.concatenate([m] * (cols // m.shape[1]), axis=1)


def denoise_kernel(shared, x_ref, te_ref, dx_ref, de_ref, win_ref, bin_ref, wmid_ref, bmid_ref, wout_ref, bout_ref,
                   out_ref, w0, w1, w2, bias, bias_out, s0h, s0l, s1h, s1l, acc):
    states, chans, rows, cols = out_ref.shape
    hid = wmid_ref.shape[2]
    fields = x_ref.shape[0]
    ext = rows + 2 * HALO
    space = lax.axis_index("space")
    height = rows * lax.axis_size("space")
    base = space * rows

    hi, lo = split(win_ref[...])
    w0[0:hid, :] = hi
    w0[hid:2 * hid, :] = lo
    for a in range(3):
        for b in range(3):
            hi, lo = split(wmid_ref[a, b])
            k = (a * 3 + b) * hid
            w1[0:hid, k:k + hid] = hi
            w1[hid:2 * hid, k:k + hid] = lo
    taps = 9 * chans
    for b in range(3):
        for a in range(3):
            hi, lo = split(wout_ref[a, b])
            m = (b * 3 + 2 - a) * chans
            w2[m:m + chans, 0:hid] = hi
            w2[m:m + chans, hid:2 * hid] = hi
            w2[taps + m:taps + m + chans, 0:hid] = lo
            w2[taps + m:taps + m + chans, hid:2 * hid] = lo
    for t in range(states):
        bias[t] = column(bin_ref[...] + te_ref[t:t + 1, :], 128)
    bias[states] = column(bmid_ref[...], 128)

    for t in range(fields):
        for r in range(ext):
            parts = shifted(x_ref[t, :, r, :])
            for b in range(3):
                hi, lo = split(parts[b])
                at = r * 3 * chans + b * chans
                s0h[t, at:at + chans, :] = hi
                s0l[t, at:at + chans, :] = lo
    acc[...] = jnp.zeros_like(acc)

    def first(r):
        k0 = 3 * chans
        at = pl.multiple_of(r * k0, 16)
        grow = base + r - (HALO - 1)
        keep = jnp.where((grow >= 0) & (grow < height), 1.0, 0.0).astype(F32)
        for t in range(states):
            if t < fields:
                f = dot(w0[...], s0h[t, pl.ds(at, 3 * k0), :])
                pre = f[:hid] + f[hid:] + dot(w0[0:hid, :], s0l[t, pl.ds(at, 3 * k0), :])
            h = silu(pre + wide(bias[t], cols)) * keep
            parts = shifted(h)
            for b in range(3):
                hi, lo = split(parts[b])
                to = pl.multiple_of(r * 3 * hid + b * hid, 128)
                s1h[t, pl.ds(to, hid), :] = hi
                s1l[t, pl.ds(to, hid), :] = lo

    def second(q):
        k1 = 3 * hid
        at = pl.multiple_of(q * k1, 128)
        grow = base + q - (HALO - 2)
        keep = jnp.where((grow >= 0) & (grow < height), 1.0, 0.0).astype(F32)
        for t in range(states):
            f = dot(w1[...], s1h[t, pl.ds(at, 3 * k1), :])
            pre = f[:hid] + f[hid:] + dot(w1[0:hid, :], s1l[t, pl.ds(at, 3 * k1), :])
            h = silu(pre + wide(bias[states], cols)) * keep
            hi, lo = split(h)
            g = dot(w2[...], jnp.concatenate([hi, lo], axis=0))
            g = g[:taps] + g[taps:]
            third = taps // 3
            left, _, _ = shifted(g[:third])
            _, _, right = shifted(g[2 * third:])
            to = pl.multiple_of(q * chans, 16)
            acc[t, pl.ds(to, third), :] += left + g[third:2 * third] + right

    def lap0(r, c):
        first(r)
        return c

    def lap(r, c):
        second(r - 3)
        first(r)
        return c

    lax.fori_loop(0, 3, lap0, 0)
    lax.fori_loop(3, rows + 4, lap, 0)
    second(rows + 1)

    for h in range(rows):
        total = None
        for t in range(states):
            noise = acc[t, (h + 2) * chans:(h + 3) * chans, :] + wide(bout_ref[...], cols)
            d = dx_ref[t] * x_ref[min(t, fields - 1), :, h + HALO, :] + de_ref[t] * noise
            total = d if total is None else total + d
            out_ref[t, :, h, :] = total


def denoise(x, te, dx, de, win, bin_, wmid, bmid, wout, bout, rows):
    fields, chans, ext, cols = x.shape
    states = te.shape[0]
    hid = wmid.shape[2]
    vm = pl.BlockSpec(memory_space=pltpu.VMEM)
    sm = pl.BlockSpec(memory_space=pltpu.SMEM)
    return pl.pallas_call(
        functools.partial(denoise_kernel, fields == 1),
        out_shape=jax.ShapeDtypeStruct((states, chans, rows, cols), F32),
        in_specs=[vm, vm, sm, sm, vm, vm, vm, vm, vm, vm],
        out_specs=vm,
        scratch_shapes=[
            pltpu.VMEM((2 * hid, 9 * chans), BF),
            pltpu.VMEM((2 * hid, 9 * hid), BF),
            pltpu.VMEM((18 * chans, 2 * hid), BF),
            pltpu.VMEM((states + 1, hid, 128), F32),
            pltpu.VMEM((chans, 128), F32),
            pltpu.VMEM((fields, ext * 3 * chans, cols), BF),
            pltpu.VMEM((fields, ext * 3 * chans, cols), BF),
            pltpu.VMEM((states, (rows + 4) * 3 * hid, cols), BF),
            pltpu.VMEM((states, (rows + 4) * 3 * hid, cols), BF),
            pltpu.VMEM((states, (rows + 4) * chans, cols), F32),
        ],
        compiler_params=pltpu.CompilerParams(vmem_limit_bytes=40 * 1024 * 1024),
        name="denoise",
    )(x, te, dx, de, win, bin_, wmid, bmid, wout, bout)


def halo_rows(v, dim):
    count = lax.axis_size("space")
    n = v.shape[dim]
    head = lax.slice_in_dim(v, 0, HALO, axis=dim)
    tail = lax.slice_in_dim(v, n - HALO, n, axis=dim)
    up = lax.ppermute(tail, "space", [(i, i + 1) for i in range(count - 1)])
    down = lax.ppermute(head, "space", [(i + 1, i) for i in range(count - 1)])
    return jnp.concatenate([up, v, down], axis=dim)


def earlier_sum(v):
    count = lax.axis_size("tm")
    total = jnp.zeros_like(v)
    for j in range(1, count):
        total = total + lax.ppermute(v, "tm", [(i, i + j) for i in range(count - j)])
    return total


def on_device(start_latent, time_embed, drift_x, drift_eps, w_in, b_in, w_mid, b_mid, w_out, b_out):
    chans, rows, cols = start_latent.shape
    hid = w_mid.shape[2]
    win = jnp.transpose(w_in, (2, 0, 1, 3)).reshape(hid, 9 * chans)
    bout = jnp.broadcast_to(b_out[:, None], (chans, 128))
    weights = (win, b_in[None], w_mid, b_mid[None], w_out, bout)
    start_ext = halo_rows(start_latent, 1)
    inputs = start_ext[None]
    for iteration in range(ITERS):
        running = denoise(inputs, time_embed, drift_x, drift_eps, *weights, rows)
        if iteration + 1 < ITERS:
            run_ext = halo_rows(running, 2)
            first = start_ext + earlier_sum(run_ext[-1])
            inputs = jnp.concatenate([first[None], first[None] + run_ext[:-1]], 0)
        else:
            return (start_latent + earlier_sum(running[-1]))[None] + running


def solution(mesh):
    in_specs = (
        P("group", "space", None),
        P("tm", None),
        P("tm"),
        P("tm"),
        P(),
        P(),
        P(),
        P(),
        P(),
        P(),
    )
    out_specs = P("tm", "group", "space", None)
    return jax.shard_map(
        on_device, mesh=mesh, in_specs=in_specs, out_specs=out_specs, check_vma=False
    )
```

```python
import functools
import jax
import jax.numpy as jnp
from jax import lax
from jax.experimental import pallas as pl
from jax.experimental.pallas import tpu as pltpu
from jax.sharding import PartitionSpec as P

HALO = 3
BF = jnp.bfloat16
F32 = jnp.float32


def split(v):
    hi = v.astype(BF)
    lo = (v - hi.astype(F32)).astype(BF)
    return hi, lo


def shifted(v):
    cols = v.shape[1]
    lane = lax.broadcasted_iota(jnp.int32, v.shape, 1)
    left = jnp.where(lane == 0, 0.0, pltpu.roll(v, 1, 1))
    right = jnp.where(lane == cols - 1, 0.0, pltpu.roll(v, cols - 1, 1))
    return left, v, right


def dot(a, b):
    return jnp.dot(a, b, preferred_element_type=F32)


def silu(u):
    half = 0.5 * u
    return half + half * jnp.tanh(half)


def column(row, n):
    return jnp.transpose(jnp.broadcast_to(row, (n, row.shape[1])))


def wide(m, cols):
    return jnp.concatenate([m] * (cols // m.shape[1]), axis=1)


MESH = pl.DeviceIdType.MESH


def picard_kernel(start_ref, te_ref, dx_ref, de_ref, win_ref, bin_ref, wmid_ref, bmid_ref, wout_ref, bout_ref,
                  out_ref, w0, w1, w2, bias, s0h, s0l, s1h, s1l, acc, x0, xin, run, car, snd, run2, car2, snd2,
                  hs_send, hs_recv, hr_send, hr_recv, c_send, c_recv, f_send, f_recv):
    states, chans, rows, cols = out_ref.shape
    hid = wmid_ref.shape[2]
    ext = rows + 2 * HALO
    space, spaces = lax.axis_index("space"), lax.axis_size("space")
    tm, tms = lax.axis_index("tm"), lax.axis_size("tm")
    height = rows * spaces
    base = space * rows
    has_up, has_down = space < spaces - 1, space > 0
    has_next, has_prev = tm < tms - 1, tm > 0
    up, down, nxt, prv = {"space": space + 1}, {"space": space - 1}, {"tm": tm + 1}, {"tm": tm - 1}

    barrier = pltpu.get_barrier_semaphore()
    sides = ((has_up, up), (has_down, down), (has_next, nxt), (has_prev, prv))
    for there, who in sides:
        @pl.when(there)
        def _(who=who):
            pl.semaphore_signal(barrier, inc=1, device_id=who, device_id_type=MESH)

    for r in range(rows):
        x0[r + HALO] = start_ref[:, r, :]

    peers = sum(jnp.where(there, 1, 0) for there, _ in sides)
    pl.semaphore_wait(barrier, peers)

    def remote(src, dst, send, recv, who):
        return pltpu.make_async_remote_copy(src_ref=src, dst_ref=dst, send_sem=send, recv_sem=recv,
                                            device_id=who, device_id_type=MESH)

    def halo_pair(make, lead):
        top, tail = lead + (pl.ds(0, HALO),), lead + (pl.ds(rows, HALO),)
        first, bottom = lead + (pl.ds(HALO, HALO),), lead + (pl.ds(rows + HALO, HALO),)
        buf, send, recv = make
        go_up = remote(buf.at[tail], buf.at[top], send.at[0], recv.at[0], up)
        go_down = remote(buf.at[first], buf.at[bottom], send.at[1], recv.at[1], down)
        return go_up, go_down, top, bottom

    def halo_start(make, lead):
        go_up, go_down, top, bottom = halo_pair(make, lead)
        buf = make[0]

        @pl.when(has_up)
        def _():
            go_up.start()

        @pl.when(has_down)
        def _():
            go_down.start()

        @pl.when(jnp.logical_not(has_down))
        def _():
            buf[top] = jnp.zeros(buf.at[top].shape, F32)

        @pl.when(jnp.logical_not(has_up))
        def _():
            buf[bottom] = jnp.zeros(buf.at[bottom].shape, F32)

    def halo_wait(make, lead):
        go_up, go_down, top, bottom = halo_pair(make, lead)

        @pl.when(has_up)
        def _():
            go_up.wait_send()
            go_down.wait_recv()

        @pl.when(has_down)
        def _():
            go_down.wait_send()
            go_up.wait_recv()

    start_halo = ((x0, hs_send, hs_recv), ())
    run_halo = ((run, hr_send, hr_recv), (slice(None),))
    halo_start(*start_halo)

    hi, lo = split(win_ref[...])
    w0[0:hid, :] = hi
    w0[hid:2 * hid, :] = lo
    for a in range(3):
        for b in range(3):
            hi, lo = split(wmid_ref[a, b])
            k = (a * 3 + b) * hid
            w1[0:hid, k:k + hid] = hi
            w1[hid:2 * hid, k:k + hid] = lo
    taps = 9 * chans
    for b in range(3):
        for a in range(3):
            hi, lo = split(wout_ref[a, b])
            m = (b * 3 + 2 - a) * chans
            w2[m:m + chans, 0:hid] = hi
            w2[m:m + chans, hid:2 * hid] = hi
            w2[taps + m:taps + m + chans, 0:hid] = lo
            w2[taps + m:taps + m + chans, hid:2 * hid] = lo
    for t in range(states):
        bias[t] = column(bin_ref[...] + te_ref[t:t + 1, :], 128)
    bias[states] = column(bmid_ref[...], 128)

    def place(t, r, v):
        parts = shifted(v)
        for b in range(3):
            hi, lo = split(parts[b])
            at = r * 3 * chans + b * chans
            s0h[t, at:at + chans, :] = hi
            s0l[t, at:at + chans, :] = lo

    inner = list(range(HALO, HALO + rows))
    outer = list(range(HALO)) + list(range(HALO + rows, ext))

    def network(fields):
        acc[...] = jnp.zeros_like(acc)

        def first(r):
            k0 = 3 * chans
            at = pl.multiple_of(r * k0, 16)
            grow = base + r - (HALO - 1)
            keep = jnp.where((grow >= 0) & (grow < height), 1.0, 0.0).astype(F32)
            for t in range(states):
                if t < fields:
                    f = dot(w0[...], s0h[t, pl.ds(at, 3 * k0), :])
                    pre = f[:hid] + f[hid:] + dot(w0[0:hid, :], s0l[t, pl.ds(at, 3 * k0), :])
                h = silu(pre + wide(bias[t], cols)) * keep
                parts = shifted(h)
                for b in range(3):
                    hi, lo = split(parts[b])
                    to = pl.multiple_of(r * 3 * hid + b * hid, 128)
                    s1h[t, pl.ds(to, hid), :] = hi
                    s1l[t, pl.ds(to, hid), :] = lo

        def second(q):
            k1 = 3 * hid
            at = pl.multiple_of(q * k1, 128)
            grow = base + q - (HALO - 2)
            keep = jnp.where((grow >= 0) & (grow < height), 1.0, 0.0).astype(F32)
            for t in range(states):
                f = dot(w1[...], s1h[t, pl.ds(at, 3 * k1), :])
                pre = f[:hid] + f[hid:] + dot(w1[0:hid, :], s1l[t, pl.ds(at, 3 * k1), :])
                h = silu(pre + wide(bias[states], cols)) * keep
                hi, lo = split(h)
                g = dot(w2[...], jnp.concatenate([hi, lo], axis=0))
                g = g[:taps] + g[taps:]
                third = taps // 3
                left, _, _ = shifted(g[:third])
                _, _, right = shifted(g[2 * third:])
                to = pl.multiple_of(q * chans, 16)
                acc[t, pl.ds(to, third), :] += left + g[third:2 * third] + right

        def lap0(r, c):
            first(r)
            return c

        def lap(r, c):
            second(r - 3)
            first(r)
            return c

        lax.fori_loop(0, 3, lap0, 0)
        lax.fori_loop(3, rows + 4, lap, 0)
        second(rows + 1)

    def drifts(put, source):
        bo = wide(bout_ref[...], cols)
        for h in range(rows):
            total = None
            for t in range(states):
                noise = acc[t, (h + 2) * chans:(h + 3) * chans, :] + bo
                d = dx_ref[t] * source(t, h + HALO) + de_ref[t] * noise
                total = d if total is None else total + d
                put(t, h, total)

    def chain(car_at, snd_at, mine, send, recv):
        copy = remote(snd_at, car_at, send, recv, nxt)

        @pl.when(has_prev)
        def _():
            copy.wait_recv()

            @pl.when(has_next)
            def _():
                snd_at[...] = car_at[...] + mine[...]

        @pl.when(jnp.logical_not(has_prev))
        def _():
            car_at[...] = jnp.zeros(car_at.shape, F32)
            snd_at[...] = mine[...]

        @pl.when(has_next)
        def _():
            copy.start()
        return copy

    for r in inner:
        place(0, r, x0[r])
    halo_wait(*start_halo)
    for r in outer:
        place(0, r, x0[r])
    network(1)

    def put1(t, h, v):
        run[t, h + HALO] = v

    drifts(put1, lambda t, r: x0[r])

    pieces = [pl.ds(HALO, rows), pl.ds(0, HALO), pl.ds(HALO + rows, HALO)]
    last = states - 1
    copies = []

    def link(n):
        at = pieces[n]
        copies.append(chain(car.at[at], snd.at[at], run.at[last, at], c_send.at[n], c_recv.at[n]))

    def build(rs):
        for r in rs:
            first_in = x0[r] + car[r]
            for t in range(states):
                v = first_in if t == 0 else first_in + run[t - 1, r]
                xin[t, r] = v
                place(t, r, v)

    halo_start(*run_halo)
    link(0)
    halo_wait(*run_halo)
    link(1)
    link(2)
    build(inner)
    build(outer)
    network(states)

    def put2(t, h, v):
        run2[t, h] = v

    drifts(put2, lambda t, r: xin[t, r])
    parts = f_send.shape[0]
    size = rows // parts
    for n in range(parts):
        at = pl.ds(n * size, size)
        copies.append(chain(car2.at[at], snd2.at[at], run2.at[last, at], f_send.at[n], f_recv.at[n]))
        for h in range(n * size, (n + 1) * size):
            first_in = x0[h + HALO] + car2[h]
            for t in range(states):
                out_ref[t, :, h, :] = first_in + run2[t, h]

    @pl.when(has_next)
    def _():
        for copy in copies:
            copy.wait_send()


def picard(start, te, dx, de, win, bin_, wmid, bmid, wout, bout):
    chans, rows, cols = start.shape
    ext = rows + 2 * HALO
    states = te.shape[0]
    hid = wmid.shape[2]
    parts = 2 if rows % 2 == 0 else 1
    vm = pl.BlockSpec(memory_space=pltpu.VMEM)
    sm = pl.BlockSpec(memory_space=pltpu.SMEM)
    dma = pltpu.SemaphoreType.DMA
    return pl.pallas_call(
        picard_kernel,
        out_shape=jax.ShapeDtypeStruct((states, chans, rows, cols), F32),
        in_specs=[vm, vm, sm, sm, vm, vm, vm, vm, vm, vm],
        out_specs=vm,
        scratch_shapes=[
            pltpu.VMEM((2 * hid, 9 * chans), BF),
            pltpu.VMEM((2 * hid, 9 * hid), BF),
            pltpu.VMEM((18 * chans, 2 * hid), BF),
            pltpu.VMEM((states + 1, hid, 128), F32),
            pltpu.VMEM((states, ext * 3 * chans, cols), BF),
            pltpu.VMEM((states, ext * 3 * chans, cols), BF),
            pltpu.VMEM((states, (rows + 4) * 3 * hid, cols), BF),
            pltpu.VMEM((states, (rows + 4) * 3 * hid, cols), BF),
            pltpu.VMEM((states, (rows + 4) * chans, cols), F32),
            pltpu.VMEM((ext, chans, cols), F32),
            pltpu.VMEM((states, ext, chans, cols), F32),
            pltpu.VMEM((states, ext, chans, cols), F32),
            pltpu.VMEM((ext, chans, cols), F32),
            pltpu.VMEM((ext, chans, cols), F32),
            pltpu.VMEM((states, rows, chans, cols), F32),
            pltpu.VMEM((rows, chans, cols), F32),
            pltpu.VMEM((rows, chans, cols), F32),
            dma((2,)), dma((2,)), dma((2,)), dma((2,)), dma((3,)), dma((3,)), dma((parts,)), dma((parts,)),
        ],
        compiler_params=pltpu.CompilerParams(
            vmem_limit_bytes=48 * 1024 * 1024, collective_id=0, has_side_effects=True),
        name="picard",
    )(start, te, dx, de, win, bin_, wmid, bmid, wout, bout)


def on_device(start_latent, time_embed, drift_x, drift_eps, w_in, b_in, w_mid, b_mid, w_out, b_out):
    chans = start_latent.shape[0]
    hid = w_mid.shape[2]
    win = jnp.transpose(w_in, (2, 0, 1, 3)).reshape(hid, 9 * chans)
    bout = jnp.broadcast_to(b_out[:, None], (chans, 128))
    return picard(start_latent, time_embed, drift_x, drift_eps, win, b_in[None], w_mid, b_mid[None], w_out, bout)


def solution(mesh):
    in_specs = (
        P("group", "space", None),
        P("tm", None),
        P("tm"),
        P("tm"),
        P(),
        P(),
        P(),
        P(),
        P(),
        P(),
    )
    out_specs = P("tm", "group", "space", None)
    return jax.shard_map(
        on_device, mesh=mesh, in_specs=in_specs, out_specs=out_specs, check_vma=False
    )
```

```python
import functools
import jax
import jax.numpy as jnp
from jax import lax
from jax.experimental import pallas as pl
from jax.experimental.pallas import tpu as pltpu
from jax.sharding import PartitionSpec as P

HALO = 3
UNROLL = 4
BF = jnp.bfloat16
F32 = jnp.float32


def split(v):
    hi = v.astype(BF)
    lo = (v - hi.astype(F32)).astype(BF)
    return hi, lo


def shifted(v):
    cols = v.shape[1]
    lane = lax.broadcasted_iota(jnp.int32, v.shape, 1)
    left = jnp.where(lane == 0, 0.0, pltpu.roll(v, 1, 1))
    right = jnp.where(lane == cols - 1, 0.0, pltpu.roll(v, cols - 1, 1))
    return left, v, right


def dot(a, b):
    return jnp.dot(a, b, preferred_element_type=F32)


def silu(u):
    half = 0.5 * u
    return half + half * jnp.tanh(half)


def column(row, n):
    return jnp.transpose(jnp.broadcast_to(row, (n, row.shape[1])))


def wide(m, cols):
    return jnp.concatenate([m] * (cols // m.shape[1]), axis=1)


MESH = pl.DeviceIdType.MESH


def picard_kernel(start_ref, te_ref, dx_ref, de_ref, win_ref, bin_ref, wmid_ref, bmid_ref, wout_ref, bout_ref,
                  out_ref, w0, w1, w2, bias, s0h, s0l, s1h, s1l, h2, acc, x0, xin, run, car, snd, run2, car2, snd2,
                  hs_send, hs_recv, hr_send, hr_recv, c_send, c_recv, f_send, f_recv):
    states, chans, rows, cols = out_ref.shape
    hid = wmid_ref.shape[2]
    ext = rows + 2 * HALO
    space, spaces = lax.axis_index("space"), lax.axis_size("space")
    tm, tms = lax.axis_index("tm"), lax.axis_size("tm")
    height = rows * spaces
    base = space * rows
    has_up, has_down = space < spaces - 1, space > 0
    has_next, has_prev = tm < tms - 1, tm > 0
    up, down, nxt, prv = {"space": space + 1}, {"space": space - 1}, {"tm": tm + 1}, {"tm": tm - 1}

    barrier = pltpu.get_barrier_semaphore()
    sides = ((has_up, up), (has_down, down), (has_next, nxt), (has_prev, prv))
    for there, who in sides:
        @pl.when(there)
        def _(who=who):
            pl.semaphore_signal(barrier, inc=1, device_id=who, device_id_type=MESH)

    for r in range(rows):
        x0[r + HALO] = start_ref[:, r, :]

    peers = sum(jnp.where(there, 1, 0) for there, _ in sides)
    pl.semaphore_wait(barrier, peers)

    def remote(src, dst, send, recv, who):
        return pltpu.make_async_remote_copy(src_ref=src, dst_ref=dst, send_sem=send, recv_sem=recv,
                                            device_id=who, device_id_type=MESH)

    def halo_pair(make, lead):
        top, tail = lead + (pl.ds(0, HALO),), lead + (pl.ds(rows, HALO),)
        first, bottom = lead + (pl.ds(HALO, HALO),), lead + (pl.ds(rows + HALO, HALO),)
        buf, send, recv = make
        go_up = remote(buf.at[tail], buf.at[top], send.at[0], recv.at[0], up)
        go_down = remote(buf.at[first], buf.at[bottom], send.at[1], recv.at[1], down)
        return go_up, go_down, top, bottom

    def halo_start(make, lead):
        go_up, go_down, top, bottom = halo_pair(make, lead)
        buf = make[0]

        @pl.when(has_up)
        def _():
            go_up.start()

        @pl.when(has_down)
        def _():
            go_down.start()

        @pl.when(jnp.logical_not(has_down))
        def _():
            buf[top] = jnp.zeros(buf.at[top].shape, F32)

        @pl.when(jnp.logical_not(has_up))
        def _():
            buf[bottom] = jnp.zeros(buf.at[bottom].shape, F32)

    def halo_wait(make, lead):
        go_up, go_down, top, bottom = halo_pair(make, lead)

        @pl.when(has_up)
        def _():
            go_up.wait_send()
            go_down.wait_recv()

        @pl.when(has_down)
        def _():
            go_down.wait_send()
            go_up.wait_recv()

    start_halo = ((x0, hs_send, hs_recv), ())
    run_halo = ((run, hr_send, hr_recv), (slice(None),))
    halo_start(*start_halo)

    hi, lo = split(win_ref[...])
    w0[0:hid, :] = hi
    w0[hid:2 * hid, :] = lo
    for a in range(3):
        for b in range(3):
            hi, lo = split(wmid_ref[a, b])
            k = (a * 3 + b) * hid
            w1[0:hid, k:k + hid] = hi
            w1[hid:2 * hid, k:k + hid] = lo
    taps = 9 * chans
    for b in range(3):
        for a in range(3):
            hi, lo = split(wout_ref[a, b])
            m = (b * 3 + 2 - a) * chans
            w2[m:m + chans, 0:hid] = hi
            w2[m:m + chans, hid:2 * hid] = hi
            w2[taps + m:taps + m + chans, 0:hid] = lo
            w2[taps + m:taps + m + chans, hid:2 * hid] = lo
    for t in range(states):
        bias[t] = column(bin_ref[...] + te_ref[t:t + 1, :], 128)
    bias[states] = column(bmid_ref[...], 128)

    def place(t, r, v):
        parts = shifted(v)
        for b in range(3):
            hi, lo = split(parts[b])
            at = r * 3 * chans + b * chans
            s0h[t, at:at + chans, :] = hi
            s0l[t, at:at + chans, :] = lo

    inner = list(range(HALO, HALO + rows))
    outer = list(range(HALO)) + list(range(HALO + rows, ext))

    def network(fields):
        acc[...] = jnp.zeros_like(acc)
        k0, k1, third = 3 * chans, 3 * hid, taps // 3

        def inside(row):
            return jnp.where((base + row >= 0) & (base + row < height), 1.0, 0.0).astype(F32)

        def first_dot(t, r):
            at = pl.ds(pl.multiple_of(r * k0, 16), 3 * k0)
            f = dot(w0[...], s0h[t, at, :])
            return f[:hid] + f[hid:] + dot(w0[0:hid, :], s0l[t, at, :])

        def first_end(t, r, pre):
            h = silu(pre + wide(bias[t], cols)) * inside(r - (HALO - 1))
            parts = shifted(h)
            for b in range(3):
                hi, lo = split(parts[b])
                to = pl.ds(pl.multiple_of(r * k1 + b * hid, 128), hid)
                s1h[t][to, :] = hi
                s1l[t][to, :] = lo

        def mid_dot(t, q):
            at = pl.ds(pl.multiple_of(q * k1, 128), 3 * k1)
            f = dot(w1[...], s1h[t][at, :])
            return f[:hid] + f[hid:] + dot(w1[0:hid, :], s1l[t][at, :])

        def mid_end(t, q, pre):
            h = silu(pre + wide(bias[states], cols)) * inside(q - (HALO - 2))
            hi, lo = split(h)
            h2[t][0:hid, :] = hi
            h2[t][hid:2 * hid, :] = lo

        def last_conv(t, q):
            g = dot(w2[...], h2[t][...])
            g = g[:taps] + g[taps:]
            left, _, _ = shifted(g[:third])
            _, _, right = shifted(g[2 * third:])
            to = pl.ds(pl.multiple_of(q * chans, 16), third)
            acc[t, to, :] += left + g[third:2 * third] + right

        def stage(r, with_first=True, with_mid=True, with_last=True):
            firsts, mids = {}, {}
            for t in range(states):
                if with_first:
                    firsts[t] = first_dot(t, r) if t < fields else firsts[0]
            for t in range(states):
                if with_mid:
                    mids[t] = mid_dot(t, r - 3)
                if with_last:
                    last_conv(t, r - 4)
                if with_first:
                    first_end(t, r, firsts[t])
                if with_mid:
                    mid_end(t, r - 3, mids[t])

        def fill(r, c):
            stage(r, True, False, False)
            return c

        def lap(r, c):
            stage(r)
            return c

        lax.fori_loop(0, 3, fill, 0)
        stage(3, True, True, False)
        lax.fori_loop(4, rows + 4, lap, 0, unroll=UNROLL)
        stage(rows + 4, False, True, True)
        stage(rows + 5, False, False, True)

    def drifts(put, source):
        bo = wide(bout_ref[...], cols)
        for h in range(rows):
            total = None
            for t in range(states):
                noise = acc[t, (h + 2) * chans:(h + 3) * chans, :] + bo
                d = dx_ref[t] * source(t, h + HALO) + de_ref[t] * noise
                total = d if total is None else total + d
                put(t, h, total)

    def chain(car_at, snd_at, mine, send, recv):
        copy = remote(snd_at, car_at, send, recv, nxt)

        @pl.when(has_prev)
        def _():
            copy.wait_recv()

            @pl.when(has_next)
            def _():
                snd_at[...] = car_at[...] + mine[...]

        @pl.when(jnp.logical_not(has_prev))
        def _():
            car_at[...] = jnp.zeros(car_at.shape, F32)
            snd_at[...] = mine[...]

        @pl.when(has_next)
        def _():
            copy.start()
        return copy

    for r in inner:
        place(0, r, x0[r])
    halo_wait(*start_halo)
    for r in outer:
        place(0, r, x0[r])
    network(1)

    def put1(t, h, v):
        run[t, h + HALO] = v

    drifts(put1, lambda t, r: x0[r])

    pieces = [pl.ds(HALO, rows), pl.ds(0, HALO), pl.ds(HALO + rows, HALO)]
    last = states - 1
    copies = []

    def link(n):
        at = pieces[n]
        copies.append(chain(car.at[at], snd.at[at], run.at[last, at], c_send.at[n], c_recv.at[n]))

    def build(rs):
        for r in rs:
            first_in = x0[r] + car[r]
            for t in range(states):
                v = first_in if t == 0 else first_in + run[t - 1, r]
                xin[t, r] = v
                place(t, r, v)

    halo_start(*run_halo)
    link(0)
    halo_wait(*run_halo)
    link(1)
    link(2)
    build(inner)
    build(outer)
    network(states)

    def put2(t, h, v):
        run2[t, h] = v

    drifts(put2, lambda t, r: xin[t, r])
    parts = f_send.shape[0]
    size = rows // parts
    for n in range(parts):
        at = pl.ds(n * size, size)
        copies.append(chain(car2.at[at], snd2.at[at], run2.at[last, at], f_send.at[n], f_recv.at[n]))
        for h in range(n * size, (n + 1) * size):
            first_in = x0[h + HALO] + car2[h]
            for t in range(states):
                out_ref[t, :, h, :] = first_in + run2[t, h]

    @pl.when(has_next)
    def _():
        for copy in copies:
            copy.wait_send()


def picard(start, te, dx, de, win, bin_, wmid, bmid, wout, bout):
    chans, rows, cols = start.shape
    ext = rows + 2 * HALO
    states = te.shape[0]
    hid = wmid.shape[2]
    parts = 2 if rows % 2 == 0 else 1
    vm = pl.BlockSpec(memory_space=pltpu.VMEM)
    sm = pl.BlockSpec(memory_space=pltpu.SMEM)
    dma = pltpu.SemaphoreType.DMA
    return pl.pallas_call(
        picard_kernel,
        out_shape=jax.ShapeDtypeStruct((states, chans, rows, cols), F32),
        in_specs=[vm, vm, sm, sm, vm, vm, vm, vm, vm, vm],
        out_specs=vm,
        scratch_shapes=[
            pltpu.VMEM((2 * hid, 9 * chans), BF),
            pltpu.VMEM((2 * hid, 9 * hid), BF),
            pltpu.VMEM((18 * chans, 2 * hid), BF),
            pltpu.VMEM((states + 1, hid, 128), F32),
            pltpu.VMEM((states, ext * 3 * chans, cols), BF),
            pltpu.VMEM((states, ext * 3 * chans, cols), BF),
            [pltpu.VMEM(((rows + 4) * 3 * hid, cols), BF)] * states,
            [pltpu.VMEM(((rows + 4) * 3 * hid, cols), BF)] * states,
            [pltpu.VMEM((2 * hid, cols), BF)] * states,
            pltpu.VMEM((states, (rows + 4) * chans, cols), F32),
            pltpu.VMEM((ext, chans, cols), F32),
            pltpu.VMEM((states, ext, chans, cols), F32),
            pltpu.VMEM((states, ext, chans, cols), F32),
            pltpu.VMEM((ext, chans, cols), F32),
            pltpu.VMEM((ext, chans, cols), F32),
            pltpu.VMEM((states, rows, chans, cols), F32),
            pltpu.VMEM((rows, chans, cols), F32),
            pltpu.VMEM((rows, chans, cols), F32),
            dma((2,)), dma((2,)), dma((2,)), dma((2,)), dma((3,)), dma((3,)), dma((parts,)), dma((parts,)),
        ],
        compiler_params=pltpu.CompilerParams(
            vmem_limit_bytes=48 * 1024 * 1024, collective_id=0, has_side_effects=True),
        name="picard",
    )(start, te, dx, de, win, bin_, wmid, bmid, wout, bout)


def on_device(start_latent, time_embed, drift_x, drift_eps, w_in, b_in, w_mid, b_mid, w_out, b_out):
    chans = start_latent.shape[0]
    hid = w_mid.shape[2]
    win = jnp.transpose(w_in, (2, 0, 1, 3)).reshape(hid, 9 * chans)
    bout = jnp.broadcast_to(b_out[:, None], (chans, 128))
    return picard(start_latent, time_embed, drift_x, drift_eps, win, b_in[None], w_mid, b_mid[None], w_out, bout)


def solution(mesh):
    in_specs = (
        P("group", "space", None),
        P("tm", None),
        P("tm"),
        P("tm"),
        P(),
        P(),
        P(),
        P(),
        P(),
        P(),
    )
    out_specs = P("tm", "group", "space", None)
    return jax.shard_map(
        on_device, mesh=mesh, in_specs=in_specs, out_specs=out_specs, check_vma=False
    )
```

```python
import functools
import jax
import jax.numpy as jnp
from jax import lax
from jax.experimental import pallas as pl
from jax.experimental.pallas import tpu as pltpu
from jax.sharding import PartitionSpec as P

HALO = 3
UNROLL = 4
BF = jnp.bfloat16
F32 = jnp.float32


def split(v):
    hi = v.astype(BF)
    lo = (v - hi.astype(F32)).astype(BF)
    return hi, lo


def shifted(v):
    cols = v.shape[1]
    lane = lax.broadcasted_iota(jnp.int32, v.shape, 1)
    left = jnp.where(lane == 0, 0.0, pltpu.roll(v, 1, 1))
    right = jnp.where(lane == cols - 1, 0.0, pltpu.roll(v, cols - 1, 1))
    return left, v, right


def dot(a, b):
    return jnp.dot(a, b, preferred_element_type=F32)


def silu(u):
    half = 0.5 * u
    return half + half * jnp.tanh(half)


def column(row, n):
    return jnp.transpose(jnp.broadcast_to(row, (n, row.shape[1])))


def wide(m, cols):
    return jnp.concatenate([m] * (cols // m.shape[1]), axis=1)


MESH = pl.DeviceIdType.MESH


def picard_kernel(start_ref, te_ref, dx_ref, de_ref, win_ref, bin_ref, wmid_ref, bmid_ref, wout_ref, bout_ref,
                  out_ref, bo_ref, w0, w1, w2, bias, s0h, s0l, s1h, s1l, h2, acc, x0, xin, run, car, snd, run2, car2, snd2,
                  hs_send, hs_recv, hr_send, hr_recv, c_send, c_recv, f_send, f_recv):
    states, chans, rows, cols = out_ref.shape
    hid = wmid_ref.shape[2]
    ext = rows + 2 * HALO
    space, spaces = lax.axis_index("space"), lax.axis_size("space")
    tm, tms = lax.axis_index("tm"), lax.axis_size("tm")
    height = rows * spaces
    base = space * rows
    has_up, has_down = space < spaces - 1, space > 0
    has_next, has_prev = tm < tms - 1, tm > 0
    up, down, nxt, prv = {"space": space + 1}, {"space": space - 1}, {"tm": tm + 1}, {"tm": tm - 1}

    barrier = pltpu.get_barrier_semaphore()
    sides = ((has_up, up), (has_down, down), (has_next, nxt), (has_prev, prv))
    for there, who in sides:
        @pl.when(there)
        def _(who=who):
            pl.semaphore_signal(barrier, inc=1, device_id=who, device_id_type=MESH)

    for r in range(rows):
        x0[r + HALO] = start_ref[:, r, :]

    peers = sum(jnp.where(there, 1, 0) for there, _ in sides)
    pl.semaphore_wait(barrier, peers)

    def remote(src, dst, send, recv, who):
        return pltpu.make_async_remote_copy(src_ref=src, dst_ref=dst, send_sem=send, recv_sem=recv,
                                            device_id=who, device_id_type=MESH)

    def halo_pair(make, lead):
        top, tail = lead + (pl.ds(0, HALO),), lead + (pl.ds(rows, HALO),)
        first, bottom = lead + (pl.ds(HALO, HALO),), lead + (pl.ds(rows + HALO, HALO),)
        buf, send, recv = make
        go_up = remote(buf.at[tail], buf.at[top], send.at[0], recv.at[0], up)
        go_down = remote(buf.at[first], buf.at[bottom], send.at[1], recv.at[1], down)
        return go_up, go_down, top, bottom

    def halo_start(make, lead):
        go_up, go_down, top, bottom = halo_pair(make, lead)
        buf = make[0]

        @pl.when(has_up)
        def _():
            go_up.start()

        @pl.when(has_down)
        def _():
            go_down.start()

        @pl.when(jnp.logical_not(has_down))
        def _():
            buf[top] = jnp.zeros(buf.at[top].shape, F32)

        @pl.when(jnp.logical_not(has_up))
        def _():
            buf[bottom] = jnp.zeros(buf.at[bottom].shape, F32)

    def halo_wait(make, lead):
        go_up, go_down, top, bottom = halo_pair(make, lead)

        @pl.when(has_up)
        def _():
            go_up.wait_send()
            go_down.wait_recv()

        @pl.when(has_down)
        def _():
            go_down.wait_send()
            go_up.wait_recv()

    start_halo = ((x0, hs_send, hs_recv), ())
    run_halo = ((run, hr_send, hr_recv), (slice(None),))
    halo_start(*start_halo)

    hi, lo = split(jnp.transpose(win_ref[...]))
    w0[0:hid, :] = hi
    w0[hid:2 * hid, :] = lo
    bias_out = column(bout_ref[...], 128)
    bo_ref[...] = bias_out
    for a in range(3):
        for b in range(3):
            hi, lo = split(wmid_ref[a, b])
            k = (a * 3 + b) * hid
            w1[0:hid, k:k + hid] = hi
            w1[hid:2 * hid, k:k + hid] = lo
    taps = 9 * chans
    for b in range(3):
        for a in range(3):
            hi, lo = split(wout_ref[a, b])
            m = (b * 3 + 2 - a) * chans
            w2[m:m + chans, 0:hid] = hi
            w2[m:m + chans, hid:2 * hid] = hi
            w2[taps + m:taps + m + chans, 0:hid] = lo
            w2[taps + m:taps + m + chans, hid:2 * hid] = lo
    for t in range(states):
        bias[t] = column(bin_ref[...] + te_ref[t:t + 1, :], 128)
    bias[states] = column(bmid_ref[...], 128)

    def place(t, r, v):
        parts = shifted(v)
        for b in range(3):
            hi, lo = split(parts[b])
            at = r * 3 * chans + b * chans
            s0h[t, at:at + chans, :] = hi
            s0l[t, at:at + chans, :] = lo

    inner = list(range(HALO, HALO + rows))
    outer = list(range(HALO)) + list(range(HALO + rows, ext))

    def network(fields):
        acc[...] = jnp.zeros_like(acc)
        k0, k1, third = 3 * chans, 3 * hid, taps // 3

        def inside(row):
            return jnp.where((base + row >= 0) & (base + row < height), 1.0, 0.0).astype(F32)

        def first_dot(t, r):
            at = pl.ds(pl.multiple_of(r * k0, 16), 3 * k0)
            f = dot(w0[...], s0h[t, at, :])
            return f[:hid] + f[hid:] + dot(w0[0:hid, :], s0l[t, at, :])

        def first_end(t, r, pre):
            h = silu(pre + wide(bias[t], cols)) * inside(r - (HALO - 1))
            parts = shifted(h)
            for b in range(3):
                hi, lo = split(parts[b])
                to = pl.ds(pl.multiple_of(r * k1 + b * hid, 128), hid)
                s1h[t][to, :] = hi
                s1l[t][to, :] = lo

        def mid_dot(t, q):
            at = pl.ds(pl.multiple_of(q * k1, 128), 3 * k1)
            f = dot(w1[...], s1h[t][at, :])
            return f[:hid] + f[hid:] + dot(w1[0:hid, :], s1l[t][at, :])

        def mid_end(t, q, pre):
            h = silu(pre + wide(bias[states], cols)) * inside(q - (HALO - 2))
            hi, lo = split(h)
            h2[t][0:hid, :] = hi
            h2[t][hid:2 * hid, :] = lo

        def last_conv(t, q):
            g = dot(w2[...], h2[t][...])
            g = g[:taps] + g[taps:]
            left, _, _ = shifted(g[:third])
            _, _, right = shifted(g[2 * third:])
            to = pl.ds(pl.multiple_of(q * chans, 16), third)
            acc[t, to, :] += left + g[third:2 * third] + right

        def stage(r, with_first=True, with_mid=True, with_last=True):
            firsts, mids = {}, {}
            for t in range(states):
                if with_first:
                    firsts[t] = first_dot(t, r) if t < fields else firsts[0]
            for t in range(states):
                if with_mid:
                    mids[t] = mid_dot(t, r - 3)
                if with_last:
                    last_conv(t, r - 4)
                if with_first:
                    first_end(t, r, firsts[t])
                if with_mid:
                    mid_end(t, r - 3, mids[t])

        def fill(r, c):
            stage(r, True, False, False)
            return c

        def lap(r, c):
            stage(r)
            return c

        lax.fori_loop(0, 3, fill, 0, unroll=3)
        stage(3, True, True, False)
        lax.fori_loop(4, rows + 4, lap, 0, unroll=UNROLL)
        stage(rows + 4, False, True, True)
        stage(rows + 5, False, False, True)

    def drifts(put, source):
        bo = wide(bo_ref[...], cols)
        for h in range(rows):
            total = None
            for t in range(states):
                noise = acc[t, (h + 2) * chans:(h + 3) * chans, :] + bo
                d = dx_ref[t] * source(t, h + HALO) + de_ref[t] * noise
                total = d if total is None else total + d
                put(t, h, total)

    def chain(car_at, snd_at, mine, send, recv):
        copy = remote(snd_at, car_at, send, recv, nxt)

        @pl.when(has_prev)
        def _():
            copy.wait_recv()

            @pl.when(has_next)
            def _():
                snd_at[...] = car_at[...] + mine[...]

        @pl.when(jnp.logical_not(has_prev))
        def _():
            car_at[...] = jnp.zeros(car_at.shape, F32)
            snd_at[...] = mine[...]

        @pl.when(has_next)
        def _():
            copy.start()
        return copy

    for r in inner:
        place(0, r, x0[r])
    halo_wait(*start_halo)
    for r in outer:
        place(0, r, x0[r])
    network(1)

    def put1(t, h, v):
        run[t, h + HALO] = v

    drifts(put1, lambda t, r: x0[r])

    pieces = [pl.ds(HALO, rows), pl.ds(0, HALO), pl.ds(HALO + rows, HALO)]
    last = states - 1
    copies = []

    def link(n):
        at = pieces[n]
        copies.append(chain(car.at[at], snd.at[at], run.at[last, at], c_send.at[n], c_recv.at[n]))

    def build(rs):
        for r in rs:
            first_in = x0[r] + car[r]
            for t in range(states):
                v = first_in if t == 0 else first_in + run[t - 1, r]
                xin[t, r] = v
                place(t, r, v)

    halo_start(*run_halo)
    link(0)
    halo_wait(*run_halo)
    link(1)
    link(2)
    build(inner)
    build(outer)
    network(states)

    def put2(t, h, v):
        run2[t, h] = v

    drifts(put2, lambda t, r: xin[t, r])
    parts = f_send.shape[0]
    size = rows // parts
    for n in range(parts):
        at = pl.ds(n * size, size)
        copies.append(chain(car2.at[at], snd2.at[at], run2.at[last, at], f_send.at[n], f_recv.at[n]))
        for h in range(n * size, (n + 1) * size):
            first_in = x0[h + HALO] + car2[h]
            for t in range(states):
                out_ref[t, :, h, :] = first_in + run2[t, h]

    @pl.when(has_next)
    def _():
        for copy in copies:
            copy.wait_send()


def picard(start, te, dx, de, win, bin_, wmid, bmid, wout, bout):
    chans, rows, cols = start.shape
    ext = rows + 2 * HALO
    states = te.shape[0]
    hid = wmid.shape[2]
    parts = 2 if rows % 2 == 0 else 1
    vm = pl.BlockSpec(memory_space=pltpu.VMEM)
    sm = pl.BlockSpec(memory_space=pltpu.SMEM)
    dma = pltpu.SemaphoreType.DMA
    return pl.pallas_call(
        picard_kernel,
        out_shape=jax.ShapeDtypeStruct((states, chans, rows, cols), F32),
        in_specs=[vm, vm, sm, sm, vm, vm, vm, vm, vm, vm],
        out_specs=vm,
        scratch_shapes=[
            pltpu.VMEM((chans, 128), F32),
            pltpu.VMEM((2 * hid, 9 * chans), BF),
            pltpu.VMEM((2 * hid, 9 * hid), BF),
            pltpu.VMEM((18 * chans, 2 * hid), BF),
            pltpu.VMEM((states + 1, hid, 128), F32),
            pltpu.VMEM((states, ext * 3 * chans, cols), BF),
            pltpu.VMEM((states, ext * 3 * chans, cols), BF),
            [pltpu.VMEM(((rows + 4) * 3 * hid, cols), BF)] * states,
            [pltpu.VMEM(((rows + 4) * 3 * hid, cols), BF)] * states,
            [pltpu.VMEM((2 * hid, cols), BF)] * states,
            pltpu.VMEM((states, (rows + 4) * chans, cols), F32),
            pltpu.VMEM((ext, chans, cols), F32),
            pltpu.VMEM((states, ext, chans, cols), F32),
            pltpu.VMEM((states, ext, chans, cols), F32),
            pltpu.VMEM((ext, chans, cols), F32),
            pltpu.VMEM((ext, chans, cols), F32),
            pltpu.VMEM((states, rows, chans, cols), F32),
            pltpu.VMEM((rows, chans, cols), F32),
            pltpu.VMEM((rows, chans, cols), F32),
            dma((2,)), dma((2,)), dma((2,)), dma((2,)), dma((3,)), dma((3,)), dma((parts,)), dma((parts,)),
        ],
        compiler_params=pltpu.CompilerParams(
            vmem_limit_bytes=48 * 1024 * 1024, collective_id=0, has_side_effects=True),
        name="picard",
    )(start, te, dx, de, win, bin_, wmid, bmid, wout, bout)


def on_device(start_latent, time_embed, drift_x, drift_eps, w_in, b_in, w_mid, b_mid, w_out, b_out):
    hid, chans = w_in.shape[2:]
    w_in = jnp.transpose(w_in, (0, 1, 3, 2)).reshape(9 * chans, hid)
    return picard(start_latent, time_embed, drift_x, drift_eps, w_in, b_in[None], w_mid, b_mid[None], w_out, b_out[None])


def solution(mesh):
    in_specs = (
        P("group", "space", None),
        P("tm", None),
        P("tm"),
        P("tm"),
        P(),
        P(),
        P(),
        P(),
        P(),
        P(),
    )
    out_specs = P("tm", "group", "space", None)
    return jax.shard_map(
        on_device, mesh=mesh, in_specs=in_specs, out_specs=out_specs, check_vma=False
    )
```
